256 devices in a mesh: layer: 8 (over z_hi, core), dict: 32 (over x, y, z_lo).
Axes of the slice: x: 4, y: 4, z: 8 (z_hi: 4, z_lo: 2; z = z_hi * 2 + z_lo), core: 2. Of those that a mesh axis runs over, the one named last changes fastest.
Arguments:
- hidden: bfloat16 [8, 512, 9216], P('layer', None, 'dict'), may hold values from -6 to 6
- row_list: int32 [512], replicated, may hold values from 0 to 511, each once
- w_down: bfloat16 [8, 9216, 2304], P('layer', 'dict'), may hold values from -0.0625 to 0.0625
- w_enc: bfloat16 [8, 2304, 16384], P('layer', None, 'dict'), may hold values from -0.046875 to 0.046875
- b_enc: float32 [16384], P('dict'), may hold values from -3 to 3
- w_dec: float32 [8, 16384, 2304], P('layer', 'dict'), may hold values from -0.046875 to 0.046875
- b_dec: float32 [8, 2304], P('layer'), may hold values from -3 to 3
- alive_mask: int32 [16384], P('dict'), may hold values 0 or 1
Outputs:
- latent: bfloat16 [512, 16384], P('layer', 'dict')
- residual: float32 [8, 512, 2304], P('layer', 'dict')
- adjoint: float32 [512, 16384], P('layer', 'dict')
The draws below stay inside these ranges and needn't reach their ends.
Inputs may be any that keep to these rules, and one draw needn't show every extreme that they name: `row_list`: a permutation of the 512 buffer rows.
All inputs are finite; a program needn't handle non-finite values. No bound on the sum of `alive_mask` on one device may be relied on, other than what follows from the above.
Results may differ from the reference program's by a relative error of at most 0.0045.
Values may be sent and summed in bfloat16 or wider, within the bound.
No kernel may reach another device: no remote copies, remote signals or barrier semaphores. Data moves between devices by JAX's collectives and lax.ppermute only.
A program may use at most 64 MiB of HBM per device.

```python
import jax
import jax.numpy as jnp
from jax import lax

D = 2304
FF = 9216
ROWS = 512
LAYERS = 8
LATENTS = 16384


def plant(entries, stream_key, smallest, high):
    index_at = [jax.random.randint(jax.random.fold_in(stream_key, axis), (), 0, length) for axis, length in enumerate(entries.shape)]
    main_axis = entries.shape.index(max(entries.shape))
    beside = index_at[:main_axis] + [(index_at[main_axis] + 1) % entries.shape[main_axis]] + index_at[main_axis + 1:]
    return entries.at[tuple(index_at)].set(smallest).at[tuple(beside)].set(high)


def level_of(key, extent, cuts, low, high):
    level, own = 1.0, jax.random.fold_in(key, 6)
    for position, blocks in cuts:
        steps = jnp.exp(jax.random.uniform(jax.random.fold_in(own, position), (blocks,), jnp.float32, low / len(cuts), high / len(cuts)))
        level = level * jnp.repeat(steps, extent[position] // blocks).reshape([-1 if axis == position else 1 for axis in range(len(extent))])
    return level


def noise(own_key, shape, width, most, split=(), held_as=jnp.bfloat16):
    gain = level_of(own_key, shape, split, -0.22, 0.18) if split else 1.0
    array = jax.random.normal(own_key, shape, jnp.float32) * width * gain
    return jnp.minimum(jnp.maximum(array, -most), most).astype(held_as)


def setup_inputs(seed: int = 0) -> dict:
    streams_of = jax.random.split(jax.random.key(seed), 9)
    hidden = noise(streams_of[0], (LAYERS, ROWS, FF), 1.0, 6.0, ((0, 8), (2, 32)))
    row_list = jax.random.permutation(streams_of[1], ROWS).astype(jnp.int32)
    w_down = noise(streams_of[2], (LAYERS, FF, D), FF ** -0.5, 0.0625, ((0, 8), (1, 32)))
    w_enc = noise(streams_of[3], (LAYERS, D, LATENTS), (D * LAYERS) ** -0.5, 0.046875, ((0, 8), (2, 32)))
    b_enc = noise(streams_of[4], (LATENTS,), 0.5, 3.0, ((0, 32),), jnp.float32)
    w_dec = noise(streams_of[5], (LAYERS, LATENTS, D), LATENTS ** -0.5, 0.046875, ((0, 8), (1, 32)), jnp.float32)
    b_dec = noise(streams_of[6], (LAYERS, D), 0.5, 3.0, ((0, 8),), jnp.float32)
    alive_mask = plant((jax.random.randint(streams_of[7], (LATENTS,), 0, 8) < 7).astype(jnp.int32), jax.random.fold_in(streams_of[7], 1), 0, 1)
    return dict(hidden=hidden, row_list=row_list, w_down=w_down, w_enc=w_enc, b_enc=b_enc, w_dec=w_dec, b_dec=b_dec, alive_mask=alive_mask)


def reference(hidden, row_list, w_down, w_enc, b_enc, w_dec, b_dec, alive_mask):
    alive_float = alive_mask.astype(jnp.float32)
    activations = []
    preact = jnp.zeros((ROWS, LATENTS), jnp.float32) + b_enc.astype(jnp.float32)
    for source in range(LAYERS):
        chosen = jnp.take(hidden[source], row_list, axis=0)
        produced = jnp.dot(chosen, w_down[source], preferred_element_type=jnp.float32).astype(jnp.bfloat16)
        activations.append(produced)
        preact = preact + jnp.dot(produced, w_enc[source], preferred_element_type=jnp.float32)
    latent = (jnp.maximum(preact, 0.0) * alive_float).astype(jnp.bfloat16)
    latent_wide = latent.astype(jnp.float32)
    residuals = []
    summed = jnp.zeros((ROWS, LATENTS), jnp.float32)
    for source in range(LAYERS):
        rebuilt = jnp.dot(latent_wide, w_dec[source], precision=lax.Precision.HIGHEST, preferred_element_type=jnp.float32) + b_dec[source]
        remainder = activations[source].astype(jnp.float32) - rebuilt
        residuals.append(remainder)
        summed = summed + jnp.dot(remainder, w_dec[source].T, precision=lax.Precision.HIGHEST, preferred_element_type=jnp.float32)
    adjoint = -summed * alive_float
    return latent, jnp.stack(residuals), adjoint
```

```python
import jax
import jax.numpy as jnp
from jax import lax
from jax.sharding import PartitionSpec as P


F32 = jnp.float32
BF16 = jnp.bfloat16
AXES = ("layer", "dict")


def where_is(i):
    l, d = divmod(i, 32)
    return l >> 1, l & 1, d >> 3, (d >> 1) & 3, d & 1


def number_of(zh, c, x, y, z):
    return (zh * 2 + c) * 32 + x * 8 + y * 2 + z


def swap(value, partner):
    pairs = [(i, number_of(*partner(*where_is(i)))) for i in range(256)]
    return lax.ppermute(value, AXES, pairs)


def along_u(d):
    return lambda zh, c, x, y, z: (zh, c, x ^ d, y, z) if c == 0 else (zh, c, x, y ^ d, z)


def along_v(d):
    return lambda zh, c, x, y, z: (zh, c, x, y ^ d, z) if c == 0 else (zh, c, x ^ d, y, z)


def along_z(zh, c, x, y, z):
    return (zh, c, x, y, z ^ 1)


def along_core(zh, c, x, y, z):
    return (zh, c ^ 1, x, y, z)


def along_zh(d):
    return lambda zh, c, x, y, z: (zh ^ d, c, x, y, z)


ORDER = (1, 3, 2)


def dot(a, b):
    return jnp.dot(a, b, preferred_element_type=F32)


def scatter_sum(part):
    sent = [swap(part(d).astype(BF16), along_u(d)) for d in ORDER]
    total = part(0)
    for got in sent:
        total = total + got.astype(F32)
    n = total.shape[0] // 4
    sent = [swap(total[d * n:(d + 1) * n].astype(BF16), along_v(d)) for d in ORDER]
    total = total[:n]
    for got in sent:
        total = total + got.astype(F32)
    n = n // 2
    return total[:n] + swap(total[n:], along_z)


def gather_rows(own):
    two = jnp.concatenate([own, swap(own, along_z)], 0)
    got = {d: swap(two, along_v(d)) for d in ORDER}
    got[0] = two
    eight = jnp.concatenate([got[d] for d in range(4)], 0)
    out = {d: swap(eight, along_u(d)) for d in ORDER}
    out[0] = eight
    return out


def turn(a):
    r, n = a.shape
    return a.reshape(4, 4, r // 16, n).transpose(1, 0, 2, 3).reshape(r, n)


def layer_sum(blocks, c, t):
    full = jnp.concatenate([blocks[d] for d in range(4)], 0)
    half = full.shape[1] // 2
    mine = lax.dynamic_slice_in_dim(full, c * half, half, 1)
    other = lax.dynamic_slice_in_dim(full, (1 - c) * half, half, 1)
    got = swap(other, along_core)
    first = jnp.where(c == 0, mine, got)
    second = jnp.where(c == 0, got, mine)
    both = first + turn(second)
    n = both.shape[0] // 4

    def block(d):
        return lax.dynamic_slice_in_dim(both, (t ^ d) * n, n, 0)

    sent = [swap(block(d).astype(BF16), along_zh(d)) for d in ORDER]
    total = block(0)
    for got in sent:
        total = total + got.astype(F32)
    return total


def per_device(hidden, row_list, w_down, w_enc, b_enc, w_dec, b_dec, alive_mask):
    hidden, w_down, w_enc, w_dec = hidden[0], w_down[0], w_enc[0], w_dec[0]
    rows = hidden.shape[0]
    share = rows // 32
    l, i = lax.axis_index("layer"), lax.axis_index("dict")
    zh, c = l >> 1, l & 1
    x, y, z = i >> 3, (i >> 1) & 3, i & 1
    t = zh ^ x

    p = lax.iota(jnp.int32, rows)
    block = p // share
    du, dv, dz = block >> 3, (block >> 1) & 3, block & 1
    dx, dy = jnp.where(c == 0, du, dv), jnp.where(c == 0, dv, du)
    place = (((dx ^ x) * 8) + ((dy ^ y) * 2) + (dz ^ z)) * share + p % share
    ids = jnp.sum(jnp.where(place[:, None] == p[None, :], row_list[None, :], 0), axis=1)
    pick = (ids[:, None] == p[None, :]).astype(BF16)
    chosen = dot(pick, hidden).astype(BF16)

    n = rows // 4
    acts_own = scatter_sum(lambda d: dot(chosen[d * n:(d + 1) * n], w_down))
    acts = gather_rows(acts_own.astype(BF16))
    preact = layer_sum({d: dot(acts[d], w_enc) for d in range(4)}, c, t)

    half = preact.shape[1]
    alive = alive_mask.astype(F32)
    alive_half = lax.dynamic_slice_in_dim(alive, c * half, half, 0)
    bias_half = lax.dynamic_slice_in_dim(b_enc, c * half, half, 0)
    lat = (jnp.maximum(preact + bias_half, 0.0) * alive_half).astype(BF16)
    pieces = [lat] + [None] * 3
    for d in ORDER:
        pieces[d] = swap(lat, along_zh(d))
    side = jnp.concatenate(pieces, 0)
    other = swap(side, along_core)
    wide = jnp.where(c == 0, jnp.concatenate([side, other], 1), jnp.concatenate([other, side], 1))
    latent_own = wide[:n].reshape(2, 2, 2, share, -1)
    latent_own = lax.dynamic_index_in_dim(latent_own, c ^ (y >> 1), 0, keepdims=False)

    def in_place(a):
        a = jnp.where((y & 1) == 0, a, a[::-1])
        a = jnp.where(z == 0, a, a[:, ::-1])
        return a.reshape(4 * share, -1)

    latent_out = in_place(latent_own)
    by_x = jnp.concatenate([lax.dynamic_slice_in_dim(wide, (t ^ d) * n, n, 0) for d in range(4)], 0)
    by_u = jnp.where(c == 0, by_x, turn(by_x))

    dec = w_dec.astype(BF16)
    rebuilt = scatter_sum(lambda d: dot(by_u[d * n:(d + 1) * n], dec))
    residual = acts_own.astype(BF16).astype(F32) - (rebuilt + b_dec)
    remainder = gather_rows(residual.astype(BF16))
    terms = {d: lax.dot_general(remainder[d], dec, (((1,), (1,)), ((), ())), preferred_element_type=F32) for d in range(4)}
    summed = layer_sum(terms, c, t) * -alive_half
    summed = summed.reshape(2, 2, 2, share, half)
    keep = lax.dynamic_index_in_dim(summed, c ^ (y >> 1), 0, keepdims=False)
    give = lax.dynamic_index_in_dim(summed, 1 - (c ^ (y >> 1)), 0, keepdims=False)
    got = swap(give.reshape(4 * share, half), along_core).reshape(keep.shape)
    adjoint = jnp.where(c == 0, jnp.concatenate([keep, got], -1), jnp.concatenate([got, keep], -1))
    return latent_out, residual[None], in_place(adjoint)


def solution(mesh):
    return jax.shard_map(
        per_device,
        mesh=mesh,
        in_specs=(
            P("layer", None, "dict"),
            P(),
            P("layer", "dict", None),
            P("layer", None, "dict"),
            P("dict"),
            P("layer", "dict", None),
            P("layer", None),
            P("dict"),
        ),
        out_specs=(P("layer", "dict"), P("layer", "dict", None), P("layer", "dict")),
        check_vma=False,
    )
```

```python
import jax
import jax.numpy as jnp
from jax import lax
from jax.sharding import PartitionSpec as P


F32 = jnp.float32
BF16 = jnp.bfloat16
AXES = ("layer", "dict")


def where_is(i):
    l, d = divmod(i, 32)
    return l >> 1, l & 1, d >> 3, (d >> 1) & 3, d & 1


def number_of(zh, c, x, y, z):
    return (zh * 2 + c) * 32 + x * 8 + y * 2 + z


def swap(value, partner):
    pairs = [(i, number_of(*partner(*where_is(i)))) for i in range(256)]
    return lax.ppermute(value, AXES, pairs)


def along_u(d):
    return lambda zh, c, x, y, z: (zh, c, x ^ d, y, z) if c == 0 else (zh, c, x, y ^ d, z)


def along_v(d):
    return lambda zh, c, x, y, z: (zh, c, x, y ^ d, z) if c == 0 else (zh, c, x ^ d, y, z)


def along_z(zh, c, x, y, z):
    return (zh, c, x, y, z ^ 1)


def along_core(zh, c, x, y, z):
    return (zh, c ^ 1, x, y, z)


def along_zh(d):
    return lambda zh, c, x, y, z: (zh ^ d, c, x, y, z)


ORDER = (1, 3, 2)


def dot(a, b):
    return jnp.dot(a, b, preferred_element_type=F32)


def add(a, b):
    return a + b.astype(F32)


def scatter_sum(part, last):
    far = part(4, 6).astype(BF16)
    low = swap(far[:far.shape[0] // 2], along_u(1))
    high = swap(far[far.shape[0] // 2:], along_u(3))
    one, three = part(2, 4), part(6, 8)
    h = one.shape[0] // 2
    three = jnp.concatenate([add(three[:h], low), three[h:]], 0)
    one = jnp.concatenate([one[:h], add(one[h:], high)], 0)
    got_one = swap(one.astype(BF16), along_u(1))
    got_three = swap(three.astype(BF16), along_u(3))
    total = add(add(part(0, 2), got_one), got_three)
    n = total.shape[0] // 4
    sent = [swap(total[d * n:(d + 1) * n].astype(BF16), along_v(d)) for d in ORDER]
    total = total[:n]
    for got in sent:
        total = add(total, got)
    n = n // 2
    got = swap(total.astype(last), along_z).astype(F32)
    return total + jnp.concatenate([got[n:], got[:n]], 0)


def gather_rows(two):
    got = {d: swap(two, along_v(d)) for d in ORDER}
    got[0] = two
    eight = jnp.concatenate([got[d] for d in range(4)], 0)
    one = swap(eight, along_u(1))
    three = swap(eight, along_u(3))
    h = eight.shape[0] // 2
    low = swap(three[:h], along_u(1))
    high = swap(one[h:], along_u(3))
    return [eight, one, jnp.concatenate([low, high], 0), three]


def turn(a):
    r, n = a.shape
    return a.reshape(4, 4, r // 16, n).transpose(1, 0, 2, 3).reshape(r, n)


def layer_sum(blocks, c, t):
    half = blocks[0].shape[1] // 2
    got = swap(jnp.concatenate([block[:, half:] for block in blocks], 0), along_core)
    mine = jnp.concatenate([block[:, :half] for block in blocks], 0)
    first = jnp.where(c == 0, mine, got)
    second = jnp.where(c == 0, got, mine)
    both = first + turn(second)
    n = both.shape[0] // 4

    def block(d):
        return lax.dynamic_slice_in_dim(both, (t ^ d) * n, n, 0)

    sent = [swap(block(d).astype(BF16), along_zh(d)) for d in ORDER]
    total = block(0)
    for got in sent:
        total = total + got.astype(F32)
    return total


def per_device(hidden, row_list, w_down, w_enc, b_enc, w_dec, b_dec, alive_mask):
    hidden, w_down, w_enc, w_dec = hidden[0], w_down[0], w_enc[0], w_dec[0]
    rows = hidden.shape[0]
    share = rows // 32
    l, i = lax.axis_index("layer"), lax.axis_index("dict")
    zh, c = l >> 1, l & 1
    x, y, z = i >> 3, (i >> 1) & 3, i & 1
    t = zh ^ x

    p = lax.iota(jnp.int32, rows)
    block = p // share
    du, dv, dz = block >> 3, (block >> 1) & 3, block & 1
    dx, dy = jnp.where(c == 0, du, dv), jnp.where(c == 0, dv, du)
    place = (((dx ^ x) * 8) + ((dy ^ y) * 2) + (dz ^ z)) * share + p % share
    ids = jnp.sum(jnp.where(place[:, None] == p[None, :], row_list[None, :], 0), axis=1)
    pick = (ids[:, None] == p[None, :]).astype(BF16)
    chosen = dot(pick, hidden).astype(BF16)

    n = rows // 4
    half = w_enc.shape[1] // 2

    def own_first(w, axis):
        return jnp.concatenate([lax.dynamic_slice_in_dim(w, side * half, half, axis) for side in (c, 1 - c)], axis)

    enc = own_first(w_enc, 1)
    acts_two = scatter_sum(lambda a, b: dot(chosen[a * n // 2:b * n // 2], w_down), F32).astype(BF16)
    acts = gather_rows(acts_two)
    preact = layer_sum([dot(piece, enc) for piece in acts], c, t)

    alive = alive_mask.astype(F32)
    alive_half = lax.dynamic_slice_in_dim(alive, c * half, half, 0)
    bias_half = lax.dynamic_slice_in_dim(b_enc, c * half, half, 0)
    lat = (jnp.maximum(preact + bias_half, 0.0) * alive_half).astype(BF16)
    pieces = [lat] + [None] * 3
    for d in ORDER:
        pieces[d] = swap(lat, along_zh(d))
    side = jnp.concatenate(pieces, 0)
    other = swap(side, along_core)
    wide = jnp.where(c == 0, jnp.concatenate([side, other], 1), jnp.concatenate([other, side], 1))
    latent_own = wide[:n].reshape(2, 2, 2, share, -1)
    latent_own = lax.dynamic_index_in_dim(latent_own, c ^ (y >> 1), 0, keepdims=False)

    def in_place(a):
        a = jnp.where((y & 1) == 0, a, a[::-1])
        a = jnp.where(z == 0, a, a[:, ::-1])
        return a.reshape(4 * share, -1)

    latent_out = in_place(latent_own)
    by_x = jnp.concatenate([lax.dynamic_slice_in_dim(wide, (t ^ d) * n, n, 0) for d in range(4)], 0)
    by_u = jnp.where(c == 0, by_x, turn(by_x))

    dec = w_dec.astype(BF16)
    rest = (w_dec - dec.astype(F32)).astype(BF16)
    dec_sides = [own_first(w, 0) for w in (dec, rest)]
    rebuilt = scatter_sum(lambda a, b: dot(by_u[a * n // 2:b * n // 2], dec), BF16)
    residual = acts_two.astype(F32) - (rebuilt + b_dec)
    remainder = gather_rows(residual.astype(BF16))

    def times(piece):
        high, low = [lax.dot_general(piece, w, (((1,), (1,)), ((), ())), preferred_element_type=F32) for w in dec_sides]
        return high + low

    summed = layer_sum([times(piece) for piece in remainder], c, t) * -alive_half
    summed = summed.reshape(2, 2, 2, share, half)
    keep = lax.dynamic_index_in_dim(summed, c ^ (y >> 1), 0, keepdims=False)
    give = lax.dynamic_index_in_dim(summed, 1 - (c ^ (y >> 1)), 0, keepdims=False)
    got = swap(give.reshape(4 * share, half), along_core).reshape(keep.shape)
    adjoint = jnp.where(c == 0, jnp.concatenate([keep, got], -1), jnp.concatenate([got, keep], -1))
    return latent_out, residual[None, :share], in_place(adjoint)


def solution(mesh):
    return jax.shard_map(
        per_device,
        mesh=mesh,
        in_specs=(
            P("layer", None, "dict"),
            P(),
            P("layer", "dict", None),
            P("layer", None, "dict"),
            P("dict"),
            P("layer", "dict", None),
            P("layer", None),
            P("dict"),
        ),
        out_specs=(P("layer", "dict"), P("layer", "dict", None), P("layer", "dict")),
        check_vma=False,
    )
```

```python
import jax
import jax.numpy as jnp
from jax import lax
from jax.sharding import PartitionSpec as P


F32 = jnp.float32
BF16 = jnp.bfloat16
AXES = ("layer", "dict")


def where_is(i):
    l, d = divmod(i, 32)
    return l >> 1, l & 1, d >> 3, (d >> 1) & 3, d & 1


def number_of(zh, c, x, y, z):
    return (zh * 2 + c) * 32 + x * 8 + y * 2 + z


def swap(value, partner):
    pairs = [(i, number_of(*partner(*where_is(i)))) for i in range(256)]
    return lax.ppermute(value, AXES, pairs)


def along_u(d):
    return lambda zh, c, x, y, z: (zh, c, x ^ d, y, z) if c == 0 else (zh, c, x, y ^ d, z)


def along_v(d):
    return lambda zh, c, x, y, z: (zh, c, x, y ^ d, z) if c == 0 else (zh, c, x ^ d, y, z)


def along_z(zh, c, x, y, z):
    return (zh, c, x, y, z ^ 1)


def along_core(zh, c, x, y, z):
    return (zh, c ^ 1, x, y, z)


def along_zh(d):
    return lambda zh, c, x, y, z: (zh ^ d, c, x, y, z)


ORDER = (1, 3, 2)


def dot(a, b):
    return jnp.dot(a, b, preferred_element_type=F32)


def add(a, b):
    return a + b.astype(F32)


def scatter_sum(part, last):
    sent = [swap(part(2 * d, 2 * d + 2).astype(BF16), along_u(d)) for d in ORDER]
    total = part(0, 2)
    for got in sent:
        total = add(total, got)
    n = total.shape[0] // 4
    sent = [swap(total[d * n:(d + 1) * n].astype(BF16), along_v(d)) for d in ORDER]
    total = total[:n]
    for got in sent:
        total = add(total, got)
    n = n // 2
    got = swap(total.astype(last), along_z).astype(F32)
    return total + jnp.concatenate([got[n:], got[:n]], 0)


def gather_rows(two):
    got = {d: swap(two, along_v(d)) for d in ORDER}
    got[0] = two
    eight = jnp.concatenate([got[d] for d in range(4)], 0)
    got = {d: swap(eight, along_u(d)) for d in ORDER}
    return [eight, got[1], got[2], got[3]]


def turn(a):
    r, n = a.shape
    return a.reshape(4, 4, r // 16, n).transpose(1, 0, 2, 3).reshape(r, n)


def layer_sum(blocks, c, t):
    half = blocks[0].shape[1] // 2
    got = swap(jnp.concatenate([block[:, half:] for block in blocks], 0), along_core)
    mine = jnp.concatenate([block[:, :half] for block in blocks], 0)
    first = jnp.where(c == 0, mine, got)
    second = jnp.where(c == 0, got, mine)
    both = first + turn(second)
    n = both.shape[0] // 4

    def block(d):
        return lax.dynamic_slice_in_dim(both, (t ^ d) * n, n, 0)

    sent = [swap(block(d).astype(BF16), along_zh(d)) for d in ORDER]
    total = block(0)
    for got in sent:
        total = total + got.astype(F32)
    return total


def per_device(hidden, row_list, w_down, w_enc, b_enc, w_dec, b_dec, alive_mask):
    hidden, w_down, w_enc, w_dec = hidden[0], w_down[0], w_enc[0], w_dec[0]
    rows = hidden.shape[0]
    share = rows // 32
    l, i = lax.axis_index("layer"), lax.axis_index("dict")
    zh, c = l >> 1, l & 1
    x, y, z = i >> 3, (i >> 1) & 3, i & 1
    t = zh ^ x

    p = lax.iota(jnp.int32, rows)
    block = p // share
    du, dv, dz = block >> 3, (block >> 1) & 3, block & 1
    dx, dy = jnp.where(c == 0, du, dv), jnp.where(c == 0, dv, du)
    place = (((dx ^ x) * 8) + ((dy ^ y) * 2) + (dz ^ z)) * share + p % share
    ids = jnp.sum(jnp.where(place[:, None] == p[None, :], row_list[None, :], 0), axis=1)
    pick = (ids[:, None] == p[None, :]).astype(BF16)
    chosen = dot(pick, hidden).astype(BF16)

    n = rows // 4
    half = w_enc.shape[1] // 2

    def own_first(w, axis):
        return jnp.concatenate([lax.dynamic_slice_in_dim(w, side * half, half, axis) for side in (c, 1 - c)], axis)

    enc = own_first(w_enc, 1)
    acts_two = scatter_sum(lambda a, b: dot(chosen[a * n // 2:b * n // 2], w_down), F32).astype(BF16)
    acts = gather_rows(acts_two)
    preact = layer_sum([dot(piece, enc) for piece in acts], c, t)

    alive = alive_mask.astype(F32)
    alive_half = lax.dynamic_slice_in_dim(alive, c * half, half, 0)
    bias_half = lax.dynamic_slice_in_dim(b_enc, c * half, half, 0)
    lat = (jnp.maximum(preact + bias_half, 0.0) * alive_half).astype(BF16)
    pieces = [lat] + [None] * 3
    for d in ORDER:
        pieces[d] = swap(lat, along_zh(d))
    side = jnp.concatenate(pieces, 0)
    other = swap(side, along_core)
    wide = jnp.where(c == 0, jnp.concatenate([side, other], 1), jnp.concatenate([other, side], 1))
    latent_own = wide[:n].reshape(2, 2, 2, share, -1)
    latent_own = lax.dynamic_index_in_dim(latent_own, c ^ (y >> 1), 0, keepdims=False)

    def in_place(a):
        a = jnp.where((y & 1) == 0, a, a[::-1])
        a = jnp.where(z == 0, a, a[:, ::-1])
        return a.reshape(4 * share, -1)

    latent_out = in_place(latent_own)
    by_x = jnp.concatenate([lax.dynamic_slice_in_dim(wide, (t ^ d) * n, n, 0) for d in range(4)], 0)
    by_u = jnp.where(c == 0, by_x, turn(by_x))

    dec = w_dec.astype(BF16)
    rest = (w_dec - dec.astype(F32)).astype(BF16)
    dec_sides = [own_first(w, 0) for w in (dec, rest)]
    rebuilt = scatter_sum(lambda a, b: dot(by_u[a * n // 2:b * n // 2], dec), BF16)
    residual = acts_two.astype(F32) - (rebuilt + b_dec)
    remainder = gather_rows(residual.astype(BF16))

    def times(piece):
        high, low = [lax.dot_general(piece, w, (((1,), (1,)), ((), ())), preferred_element_type=F32) for w in dec_sides]
        return high + low

    summed = layer_sum([times(piece) for piece in remainder], c, t) * -alive_half
    summed = summed.reshape(2, 2, 2, share, half)
    keep = lax.dynamic_index_in_dim(summed, c ^ (y >> 1), 0, keepdims=False)
    give = lax.dynamic_index_in_dim(summed, 1 - (c ^ (y >> 1)), 0, keepdims=False)
    got = swap(give.reshape(4 * share, half), along_core).reshape(keep.shape)
    adjoint = jnp.where(c == 0, jnp.concatenate([keep, got], -1), jnp.concatenate([got, keep], -1))
    return latent_out, residual[None, :share], in_place(adjoint)


def solution(mesh):
    return jax.shard_map(
        per_device,
        mesh=mesh,
        in_specs=(
            P("layer", None, "dict"),
            P(),
            P("layer", "dict", None),
            P("layer", None, "dict"),
            P("dict"),
            P("layer", "dict", None),
            P("layer", None),
            P("dict"),
        ),
        out_specs=(P("layer", "dict"), P("layer", "dict", None), P("layer", "dict")),
        check_vma=False,
    )
```

```python
import jax
import jax.numpy as jnp
from jax import lax
from jax.sharding import PartitionSpec as P


F32 = jnp.float32
BF16 = jnp.bfloat16
AXES = ("layer", "dict")


def where_is(i):
    l, d = divmod(i, 32)
    return l >> 1, l & 1, d >> 3, (d >> 1) & 3, d & 1


def number_of(zh, c, x, y, z):
    return (zh * 2 + c) * 32 + x * 8 + y * 2 + z


def swap(value, partner):
    pairs = [(i, number_of(*partner(*where_is(i)))) for i in range(256)]
    return lax.ppermute(value, AXES, pairs)


def swap_far(value, s):
    return swap(value, along_u(gray(s)))


def along_u(d):
    return lambda zh, c, x, y, z: (zh, c, x ^ d, y, z) if c == 0 else (zh, c, x, y ^ d, z)


def along_v(d):
    return lambda zh, c, x, y, z: (zh, c, x, y ^ d, z) if c == 0 else (zh, c, x ^ d, y, z)


def along_z(zh, c, x, y, z):
    return (zh, c, x, y, z ^ 1)


def along_core(zh, c, x, y, z):
    return (zh, c ^ 1, x, y, z)


def along_zh(d):
    return lambda zh, c, x, y, z: (zh ^ d, c, x, y, z)


def gray(s):
    return s ^ (s >> 1)


SLOTS = (1, 2, 3)


def dot(a, b):
    return jnp.dot(a, b, preferred_element_type=F32)


def add(a, b):
    return a + b.astype(F32)


def scatter_sum(part, last):
    sent = [swap_far(part(s).astype(BF16), s) for s in SLOTS]
    total = part(0)
    for got in sent:
        total = add(total, got)
    n = total.shape[0] // 4
    sent = [swap(total[s * n:(s + 1) * n].astype(BF16), along_v(gray(s))) for s in SLOTS]
    total = total[:n]
    for got in sent:
        total = add(total, got)
    n = n // 2
    got = swap(total.astype(last), along_z)
    got = got.astype(F32)
    return total + jnp.concatenate([got[n:], got[:n]], 0)


def gather_rows(two):
    eight = jnp.concatenate([two] + [swap(two, along_v(gray(s))) for s in SLOTS], 0)
    one, three, far = [swap_far(eight, s) for s in SLOTS]
    return [eight, one, three, far]


def turn(a):
    r, n = a.shape
    return a.reshape(4, 4, r // 16, n).transpose(1, 0, 2, 3).reshape(r, n)


def layer_sum(blocks, c, t):
    half = blocks[0].shape[1] // 2
    got = swap(jnp.concatenate([block[:, half:] for block in blocks], 0), along_core)
    mine = jnp.concatenate([block[:, :half] for block in blocks], 0)
    first = jnp.where(c == 0, mine, got)
    second = jnp.where(c == 0, got, mine)
    both = first + turn(second)
    n = both.shape[0] // 4

    def block(d):
        return lax.dynamic_slice_in_dim(both, gray(t ^ d) * n, n, 0)

    sent = [swap(block(gray(s)).astype(BF16), along_zh(gray(s))) for s in SLOTS]
    total = block(0)
    for got in sent:
        total = total + got.astype(F32)
    return total


def per_device(hidden, row_list, w_down, w_enc, b_enc, w_dec, b_dec, alive_mask):
    hidden, w_down, w_enc, w_dec = hidden[0], w_down[0], w_enc[0], w_dec[0]
    rows = hidden.shape[0]
    share = rows // 32
    l, i = lax.axis_index("layer"), lax.axis_index("dict")
    zh, c = l >> 1, l & 1
    x, y, z = i >> 3, (i >> 1) & 3, i & 1
    t = zh ^ x

    p = lax.iota(jnp.int32, rows)
    block = p // share
    du, dv, dz = gray(block >> 3), gray((block >> 1) & 3), block & 1
    dx, dy = jnp.where(c == 0, du, dv), jnp.where(c == 0, dv, du)
    place = (((dx ^ x) * 8) + ((dy ^ y) * 2) + (dz ^ z)) * share + p % share
    ids = jnp.sum(jnp.where(place[:, None] == p[None, :], row_list[None, :], 0), axis=1)
    pick = (ids[:, None] == p[None, :]).astype(BF16)
    chosen = dot(pick, hidden).astype(BF16)
    n = rows // 4
    half = w_enc.shape[1] // 2

    def own_first(w, axis):
        return jnp.concatenate([lax.dynamic_slice_in_dim(w, side * half, half, axis) for side in (c, 1 - c)], axis)

    enc = own_first(w_enc, 1)

    def produced(s):
        return dot(chosen[s * n:(s + 1) * n], w_down)

    acts_two = scatter_sum(produced, F32)
    acts_two = acts_two.astype(BF16)
    dec = w_dec.astype(BF16)
    rest = (w_dec - dec.astype(F32)).astype(BF16)
    dec_high, dec_low = own_first(dec, 0), own_first(rest, 0)
    acts = gather_rows(acts_two)
    first = dot(acts[0], enc)
    preact = layer_sum([first] + [dot(piece, enc) for piece in acts[1:]], c, t)

    alive = alive_mask.astype(F32)
    alive_half = lax.dynamic_slice_in_dim(alive, c * half, half, 0)
    bias_half = lax.dynamic_slice_in_dim(b_enc, c * half, half, 0)
    lat = (jnp.maximum(preact + bias_half, 0.0) * alive_half).astype(BF16)
    side = jnp.concatenate([lat] + [swap(lat, along_zh(gray(s))) for s in SLOTS], 0)
    wide = jnp.concatenate([side, swap(side, along_core)], 1)
    top = c ^ (y >> 1)

    def all_latents(a):
        return jnp.where(c == 0, a, jnp.concatenate([a[..., half:], a[..., :half]], -1))

    latent_own = lax.dynamic_index_in_dim(wide[:n].reshape(2, 2, 2, share, -1), top, 0, keepdims=False)

    def in_place(a):
        a = jnp.where(((y & 1) ^ top) == 0, a, a[::-1])
        a = jnp.where(z == 0, a, a[:, ::-1])
        return a.reshape(4 * share, -1)

    latent_out = in_place(all_latents(latent_own))
    by_x = jnp.concatenate([lax.dynamic_slice_in_dim(wide, gray(t ^ gray(s)) * n, n, 0) for s in range(4)], 0)
    by_u = jnp.where(c == 0, by_x, turn(by_x))

    rebuilt = scatter_sum(lambda s: dot(by_u[s * n:(s + 1) * n], dec_high), BF16)
    residual = acts_two.astype(F32) - (rebuilt + b_dec)
    remainder = gather_rows(residual.astype(BF16))

    def times(piece):
        high, low = [lax.dot_general(piece, w, (((1,), (1,)), ((), ())), preferred_element_type=F32) for w in (dec_high, dec_low)]
        return high + low

    first = times(remainder[0])
    summed = layer_sum([first] + [times(piece) for piece in remainder[1:]], c, t) * -alive_half
    summed = summed.reshape(2, 2, 2, share, half)
    keep = lax.dynamic_index_in_dim(summed, top, 0, keepdims=False)
    give = lax.dynamic_index_in_dim(summed, 1 - top, 0, keepdims=False)
    got = swap(give.reshape(4 * share, half), along_core).reshape(keep.shape)
    adjoint = all_latents(jnp.concatenate([keep, got], -1))
    return latent_out, residual[None, :share], in_place(adjoint)


def solution(mesh):
    return jax.shard_map(
        per_device,
        mesh=mesh,
        in_specs=(
            P("layer", None, "dict"),
            P(),
            P("layer", "dict", None),
            P("layer", None, "dict"),
            P("dict"),
            P("layer", "dict", None),
            P("layer", None),
            P("dict"),
        ),
        out_specs=(P("layer", "dict"), P("layer", "dict", None), P("layer", "dict")),
        check_vma=False,
    )
```

```python
import jax
import jax.numpy as jnp
from jax import lax
from jax.sharding import PartitionSpec as P


F32 = jnp.float32
BF16 = jnp.bfloat16
AXES = ("layer", "dict")


def where_is(i):
    l, d = divmod(i, 32)
    return l >> 1, l & 1, d >> 3, (d >> 1) & 3, d & 1


def number_of(zh, c, x, y, z):
    return (zh * 2 + c) * 32 + x * 8 + y * 2 + z


def swap(value, partner):
    pairs = [(i, number_of(*partner(*where_is(i)))) for i in range(256)]
    return lax.ppermute(value, AXES, pairs)


def swap_far(value, s):
    return swap(value, along_u(gray(s)))


def along_u(d):
    return lambda zh, c, x, y, z: (zh, c, x ^ d, y, z) if c == 0 else (zh, c, x, y ^ d, z)


def along_v(d):
    return lambda zh, c, x, y, z: (zh, c, x, y ^ d, z) if c == 0 else (zh, c, x ^ d, y, z)


def along_z(zh, c, x, y, z):
    return (zh, c, x, y, z ^ 1)


def along_core(zh, c, x, y, z):
    return (zh, c ^ 1, x, y, z)


def along_zh(d):
    return lambda zh, c, x, y, z: (zh ^ d, c, x, y, z)


def gray(s):
    return s ^ (s >> 1)


SLOTS = (1, 2, 3)


def dot(a, b):
    return jnp.dot(a, b, preferred_element_type=F32)


def add(a, b):
    return a + b.astype(F32)


def scatter_sum(part, last):
    sent = [swap_far(part(s).astype(BF16), s) for s in SLOTS]
    total = part(0)
    for got in sent:
        total = add(total, got)
    n = total.shape[0] // 4
    sent = [swap(total[s * n:(s + 1) * n].astype(BF16), along_v(gray(s))) for s in SLOTS]
    total = total[:n]
    for got in sent:
        total = add(total, got)
    n = n // 2
    got = swap(total.astype(last), along_z)
    got = got.astype(F32)
    return total + jnp.concatenate([got[n:], got[:n]], 0)


def gather_rows(two):
    eight = jnp.concatenate([two] + [swap(two, along_v(gray(s))) for s in SLOTS], 0)
    one, three, far = [swap_far(eight, s) for s in SLOTS]
    return [eight, one, three, far]


def turn(a):
    r, n = a.shape
    return a.reshape(4, 4, r // 16, n).transpose(1, 0, 2, 3).reshape(r, n)


def layer_sum(blocks, c, t):
    half = blocks[0].shape[1] // 2
    early = swap(jnp.concatenate([block[:, half:] for block in blocks[:2]], 0), along_core)
    got = jnp.concatenate([early, swap(blocks[2][:, half:], along_core)], 0)
    mine = jnp.concatenate([block[:, :half] for block in blocks], 0)
    first = jnp.where(c == 0, mine, got)
    second = jnp.where(c == 0, got, mine)
    both = first + turn(second)
    n = both.shape[0] // 4

    def block(d):
        return lax.dynamic_slice_in_dim(both, gray(t ^ d) * n, n, 0)

    sent = [swap(block(gray(s)).astype(BF16), along_zh(gray(s))) for s in SLOTS]
    total = block(0)
    for got in sent:
        total = total + got.astype(F32)
    return total


def per_device(hidden, row_list, w_down, w_enc, b_enc, w_dec, b_dec, alive_mask):
    hidden, w_down, w_enc, w_dec = hidden[0], w_down[0], w_enc[0], w_dec[0]
    rows = hidden.shape[0]
    share = rows // 32
    l, i = lax.axis_index("layer"), lax.axis_index("dict")
    zh, c = l >> 1, l & 1
    x, y, z = i >> 3, (i >> 1) & 3, i & 1
    t = zh ^ x

    p = lax.iota(jnp.int32, rows)
    block = p // share
    du, dv, dz = gray(block >> 3), gray((block >> 1) & 3), block & 1
    dx, dy = jnp.where(c == 0, du, dv), jnp.where(c == 0, dv, du)
    place = (((dx ^ x) * 8) + ((dy ^ y) * 2) + (dz ^ z)) * share + p % share
    ids = jnp.sum(jnp.where(place[:, None] == p[None, :], row_list[None, :], 0), axis=1)
    pick = (ids[:, None] == p[None, :]).astype(BF16)
    chosen = dot(pick, hidden).astype(BF16)
    n = rows // 4
    half = w_enc.shape[1] // 2

    def own_first(w, axis):
        return jnp.concatenate([lax.dynamic_slice_in_dim(w, side * half, half, axis) for side in (c, 1 - c)], axis)

    enc = own_first(w_enc, 1)

    def produced(s):
        return dot(chosen[s * n:(s + 1) * n], w_down)

    acts_two = scatter_sum(produced, F32)
    acts_two = acts_two.astype(BF16)
    dec = w_dec.astype(BF16)
    rest = (w_dec - dec.astype(F32)).astype(BF16)
    dec_high, dec_low = own_first(dec, 0), own_first(rest, 0)
    acts = gather_rows(acts_two)
    first = dot(acts[0], enc)
    preact = layer_sum([first, dot(acts[1], enc), dot(jnp.concatenate(acts[2:], 0), enc)], c, t)

    alive = alive_mask.astype(F32)
    alive_half = lax.dynamic_slice_in_dim(alive, c * half, half, 0)
    bias_half = lax.dynamic_slice_in_dim(b_enc, c * half, half, 0)
    lat = (jnp.maximum(preact + bias_half, 0.0) * alive_half).astype(BF16)
    side = jnp.concatenate([lat] + [swap(lat, along_zh(gray(s))) for s in SLOTS], 0)
    wide = jnp.concatenate([side, swap(side, along_core)], 1)
    top = c ^ (y >> 1)

    def all_latents(a):
        return jnp.where(c == 0, a, jnp.concatenate([a[..., half:], a[..., :half]], -1))

    latent_own = lax.dynamic_index_in_dim(wide[:n].reshape(2, 2, 2, share, -1), top, 0, keepdims=False)

    def in_place(a):
        a = jnp.where(((y & 1) ^ top) == 0, a, a[::-1])
        a = jnp.where(z == 0, a, a[:, ::-1])
        return a.reshape(4 * share, -1)

    latent_out = in_place(all_latents(latent_own))
    by_x = jnp.concatenate([lax.dynamic_slice_in_dim(wide, gray(t ^ gray(s)) * n, n, 0) for s in range(4)], 0)
    by_u = jnp.where(c == 0, by_x, turn(by_x))

    rebuilt = scatter_sum(lambda s: dot(by_u[s * n:(s + 1) * n], dec_high), BF16)
    residual = acts_two.astype(F32) - (rebuilt + b_dec)
    remainder = gather_rows(residual.astype(BF16))

    def times(piece):
        high, low = [lax.dot_general(piece, w, (((1,), (1,)), ((), ())), preferred_element_type=F32) for w in (dec_high, dec_low)]
        return high + low

    first = times(remainder[0])
    summed = layer_sum([first, times(remainder[1]), times(jnp.concatenate(remainder[2:], 0))], c, t) * -alive_half
    summed = summed.reshape(2, 2, 2, share, half)
    keep = lax.dynamic_index_in_dim(summed, top, 0, keepdims=False)
    give = lax.dynamic_index_in_dim(summed, 1 - top, 0, keepdims=False)
    got = swap(give.reshape(4 * share, half), along_core).reshape(keep.shape)
    adjoint = all_latents(jnp.concatenate([keep, got], -1))
    return latent_out, residual[None, :share], in_place(adjoint)


def solution(mesh):
    return jax.shard_map(
        per_device,
        mesh=mesh,
        in_specs=(
            P("layer", None, "dict"),
            P(),
            P("layer", "dict", None),
            P("layer", None, "dict"),
            P("dict"),
            P("layer", "dict", None),
            P("layer", None),
            P("dict"),
        ),
        out_specs=(P("layer", "dict"), P("layer", "dict", None), P("layer", "dict")),
        check_vma=False,
    )
```

```python
import jax
import jax.numpy as jnp
from jax import lax
from jax.sharding import PartitionSpec as P


F32 = jnp.float32
BF16 = jnp.bfloat16
AXES = ("layer", "dict")


def where_is(i):
    l, d = divmod(i, 32)
    return l >> 1, l & 1, d >> 3, (d >> 1) & 3, d & 1


def number_of(zh, c, x, y, z):
    return (zh * 2 + c) * 32 + x * 8 + y * 2 + z


def swap(value, partner):
    pairs = [(i, number_of(*partner(*where_is(i)))) for i in range(256)]
    return lax.ppermute(value, AXES, pairs)


def swap_far(value, s):
    return swap(value, along_u(gray(s)))


def along_u(d):
    return lambda zh, c, x, y, z: (zh, c, x ^ d, y, z) if c == 0 else (zh, c, x, y ^ d, z)


def along_v(d):
    return lambda zh, c, x, y, z: (zh, c, x, y ^ d, z) if c == 0 else (zh, c, x ^ d, y, z)


def along_z(zh, c, x, y, z):
    return (zh, c, x, y, z ^ 1)


def along_core(zh, c, x, y, z):
    return (zh, c ^ 1, x, y, z)


def along_zh(d):
    return lambda zh, c, x, y, z: (zh ^ d, c, x, y, z)


def gray(s):
    return s ^ (s >> 1)


SLOTS = (1, 2, 3)


def dot(a, b):
    return jnp.dot(a, b, preferred_element_type=F32)


def add(a, b):
    return a + b.astype(F32)


def scatter_sum(part, last):
    sent = [swap_far(part(s).astype(BF16), s) for s in SLOTS]
    total = part(0)
    for got in sent:
        total = add(total, got)
    n = total.shape[0] // 4
    sent = [swap(total[s * n:(s + 1) * n].astype(BF16), along_v(gray(s))) for s in SLOTS]
    total = total[:n]
    for got in sent:
        total = add(total, got)
    n = n // 2
    got = swap(total.astype(last), along_z)
    got = got.astype(F32)
    return total + jnp.concatenate([got[n:], got[:n]], 0)


def gather_rows(two):
    eight = jnp.concatenate([two] + [swap(two, along_v(gray(s))) for s in SLOTS], 0)
    one, three, far = [swap_far(eight, s) for s in SLOTS]
    return [eight, one, three, far]


def turn(a):
    r, n = a.shape
    return a.reshape(4, 4, r // 16, n).transpose(1, 0, 2, 3).reshape(r, n)


def layer_sum(blocks, c, t):
    half = blocks[0].shape[1] // 2
    early = swap(jnp.concatenate([block[:, half:] for block in blocks[:2]], 0), along_core)
    got = jnp.concatenate([early, swap(blocks[2][:, half:], along_core)], 0)
    mine = jnp.concatenate([block[:, :half] for block in blocks], 0)
    first = jnp.where(c == 0, mine, got)
    second = jnp.where(c == 0, got, mine)
    both = first + turn(second)
    n = both.shape[0] // 4

    def block(d):
        return lax.dynamic_slice_in_dim(both, gray(t ^ d) * n, n, 0)

    sent = [swap(block(gray(s)).astype(BF16), along_zh(gray(s))) for s in SLOTS]
    total = block(0)
    for got in sent:
        total = total + got.astype(F32)
    return total


def per_device(hidden, row_list, w_down, w_enc, b_enc, w_dec, b_dec, alive_mask):
    hidden, w_down, w_enc, w_dec = hidden[0], w_down[0], w_enc[0], w_dec[0]
    rows = hidden.shape[0]
    share = rows // 32
    l, i = lax.axis_index("layer"), lax.axis_index("dict")
    zh, c = l >> 1, l & 1
    x, y, z = i >> 3, (i >> 1) & 3, i & 1
    t = zh ^ x

    p = lax.iota(jnp.int32, rows)
    block = p // share
    du, dv, dz = gray(block >> 3), gray((block >> 1) & 3), block & 1
    dx, dy = jnp.where(c == 0, du, dv), jnp.where(c == 0, dv, du)
    place = (((dx ^ x) * 8) + ((dy ^ y) * 2) + (dz ^ z)) * share + p % share
    ids = jnp.sum(jnp.where(place[:, None] == p[None, :], row_list[None, :], 0), axis=1)
    pick = (ids[:, None] == p[None, :]).astype(BF16)
    chosen = dot(pick, hidden).astype(BF16)
    n = rows // 4
    half = w_enc.shape[1] // 2

    def own_first(w, axis):
        return jnp.concatenate([lax.dynamic_slice_in_dim(w, side * half, half, axis) for side in (c, 1 - c)], axis)

    enc = own_first(w_enc, 1)

    def produced(s):
        return dot(chosen[s * n:(s + 1) * n], w_down)

    acts_two = scatter_sum(produced, F32)
    acts_two = acts_two.astype(BF16)
    dec = w_dec.astype(BF16)
    rest = (w_dec - dec.astype(F32)).astype(BF16)
    dec_high, dec_low = own_first(dec, 0), own_first(rest, 0)
    acts = gather_rows(acts_two)
    first = dot(acts[0], enc)
    preact = layer_sum([first, dot(acts[1], enc), dot(jnp.concatenate(acts[2:], 0), enc)], c, t)

    alive = alive_mask.astype(F32)
    alive_half = lax.dynamic_slice_in_dim(alive, c * half, half, 0)
    bias_half = lax.dynamic_slice_in_dim(b_enc, c * half, half, 0)
    lat = (jnp.maximum(preact + bias_half, 0.0) * alive_half).astype(BF16)
    pieces = [lat] + [swap(lat, along_zh(gray(s))) for s in SLOTS]
    side = jnp.concatenate(pieces, 0)
    other = jnp.concatenate([swap(lat, along_core), swap(jnp.concatenate(pieces[1:], 0), along_core)], 0)
    wide = jnp.concatenate([side, other], 1)
    top = c ^ (y >> 1)

    def all_latents(a):
        return jnp.where(c == 0, a, jnp.concatenate([a[..., half:], a[..., :half]], -1))

    latent_own = lax.dynamic_index_in_dim(wide[:n].reshape(2, 2, 2, share, -1), top, 0, keepdims=False)

    def in_place(a):
        a = jnp.where(((y & 1) ^ top) == 0, a, a[::-1])
        a = jnp.where(z == 0, a, a[:, ::-1])
        return a.reshape(4 * share, -1)

    latent_out = in_place(all_latents(latent_own))
    by_x = jnp.concatenate([lax.dynamic_slice_in_dim(wide, gray(t ^ gray(s)) * n, n, 0) for s in range(4)], 0)
    by_u = jnp.where(c == 0, by_x, turn(by_x))

    rebuilt = scatter_sum(lambda s: dot(by_u[s * n:(s + 1) * n], dec_high), BF16)
    residual = acts_two.astype(F32) - (rebuilt + b_dec)
    remainder = gather_rows(residual.astype(BF16))

    def times(piece):
        high, low = [lax.dot_general(piece, w, (((1,), (1,)), ((), ())), preferred_element_type=F32) for w in (dec_high, dec_low)]
        return high + low

    first = times(remainder[0])
    summed = layer_sum([first, times(remainder[1]), times(jnp.concatenate(remainder[2:], 0))], c, t) * -alive_half
    summed = summed.reshape(2, 2, 2, share, half)
    keep = lax.dynamic_index_in_dim(summed, top, 0, keepdims=False)
    give = lax.dynamic_index_in_dim(summed, 1 - top, 0, keepdims=False)
    got = swap(give.reshape(4 * share, half), along_core).reshape(keep.shape)
    adjoint = all_latents(jnp.concatenate([keep, got], -1))
    return latent_out, residual[None, :share], in_place(adjoint)


def solution(mesh):
    return jax.shard_map(
        per_device,
        mesh=mesh,
        in_specs=(
            P("layer", None, "dict"),
            P(),
            P("layer", "dict", None),
            P("layer", None, "dict"),
            P("dict"),
            P("layer", "dict", None),
            P("layer", None),
            P("dict"),
        ),
        out_specs=(P("layer", "dict"), P("layer", "dict", None), P("layer", "dict")),
        check_vma=False,
    )
```
